128 devices in a mesh: cmp: 8 (over z_hi, y), tgt: 16 (over x, z_lo, core).
Axes of the slice: x: 4, y: 4, z: 4 (z_hi: 2, z_lo: 2; z = z_hi * 2 + z_lo), core: 2. Of those that a mesh axis runs over, the one named last changes fastest.
Arguments:
- affinity: bfloat16 [16384, 12288], P('cmp', 'tgt'), may hold values from -6 to 6
- comp_vectors: bfloat16 [16384, 2048], P('cmp'), may hold values from -0.046875 to 0.046875
- targ_vectors: bfloat16 [12288, 2048], P('tgt'), may hold values from -0.0546875 to 0.0546875
- comp_values: float32 [2048], P('cmp'), may hold values from 0.05 to 4
- targ_values: float32 [2048], P('tgt'), may hold values from 0.05 to 4
Outputs:
- predicted: float32 [16384, 12288], P('cmp', 'tgt')
The draws below stay inside these ranges and needn't reach their ends.
All inputs are finite; a program needn't handle non-finite values.
Results may differ from the reference program's by a relative error of at most 0.0037.
Values may be sent and summed in bfloat16 or wider, within the bound.
A program may use at most 128 MiB of HBM per device.

```python
import math
import jax
import jax.numpy as jnp
from jax import lax

NT = 12288
KT = 2048
KC = 2048
NC = 16384


def level_of(key, extent, cuts, least, top_value):
    gain, own = 1.0, jax.random.fold_in(key, 6)
    for dim, blocks in cuts:
        steps = jnp.exp(jax.random.uniform(jax.random.fold_in(own, dim), (blocks,), jnp.float32, least / len(cuts), top_value / len(cuts)))
        gain = gain * jnp.repeat(steps, extent[dim] // blocks).reshape([-1 if axis == dim else 1 for axis in range(len(extent))])
    return gain


def noise(own_key, dims, width, bound, shards=(), kind=jnp.bfloat16):
    level = level_of(own_key, dims, shards, -0.22, 0.18) if shards else 1.0
    array = jax.random.normal(own_key, dims, jnp.float32) * width * level
    return jnp.minimum(jnp.maximum(array, -bound), bound).astype(kind)


def setup_inputs(seed: int = 0) -> dict:
    arg_keys = jax.random.split(jax.random.key(seed), 6)
    affinity = noise(arg_keys[0], (NC, NT), 1.0, 6.0, ((0, 8), (1, 16)))
    comp_vectors = noise(arg_keys[1], (NC, KC), NC ** -0.5, 0.046875, ((0, 8),))
    targ_vectors = noise(arg_keys[2], (NT, KT), NT ** -0.5, 0.0546875, ((0, 16),))
    comp_values = jnp.clip(jnp.exp(math.log(4.0) - 4.3820266 * jax.random.uniform(arg_keys[3], (KC,), jnp.float32) ** level_of(arg_keys[3], (KC,), ((0, 8),), -0.2, 0.2)), 0.05, 4.0)
    targ_values = jnp.clip(jnp.exp(math.log(4.0) - 4.3820266 * jax.random.uniform(arg_keys[4], (KT,), jnp.float32) ** level_of(arg_keys[4], (KT,), ((0, 16),), -0.2, 0.2)), 0.05, 4.0)
    return {"affinity": affinity, "comp_vectors": comp_vectors, "targ_vectors": targ_vectors, "comp_values": comp_values, "targ_values": targ_values}


def reference(affinity, comp_vectors, targ_vectors, comp_values, targ_values):
    half = jnp.dot(affinity, targ_vectors, preferred_element_type=jnp.float32)
    coeffs = jnp.dot(comp_vectors.astype(jnp.float32).T, half, precision=lax.Precision.HIGHEST, preferred_element_type=jnp.float32)
    scaled = (coeffs / (comp_values[:, None] * targ_values[None, :] + 0.25)).astype(jnp.bfloat16)
    mapped = jnp.dot(comp_vectors, scaled, preferred_element_type=jnp.float32).astype(jnp.bfloat16)
    return jnp.dot(mapped, targ_vectors.T, preferred_element_type=jnp.float32)
```

```python
import functools

import jax
import jax.numpy as jnp
from jax import lax
from jax.experimental import pallas as pl
from jax.experimental.pallas import tpu as pltpu
from jax.sharding import PartitionSpec as P

MESH = pl.DeviceIdType.MESH
F32, BF16 = jnp.float32, jnp.bfloat16
CHUNKS = 2
PARTS = 3
ORDERS = ((1, 2, 4), (2, 4, 1), (4, 1, 2))
ROW_TILE = 512


def flip4(v, bits):
    return (v, v + 1 - 2 * lax.rem(v, 2), 3 - v, lax.rem(v + 2, 4))[bits]


def cmp_at(c, j):
    y = lax.rem(c, 4)
    base = c - y
    return (4 - base if j & 4 else base) + flip4(y, j & 3)


def tgt_at(t, k):
    x, z, core = t // 4, lax.rem(t // 2, 2), lax.rem(t, 2)
    z = 1 - z if k & 4 else z
    core = 1 - core if k & 8 else core
    return flip4(x, k & 3) * 4 + z * 2 + core


def block_of(p, r):
    d1, d2, d3 = ORDERS[p]
    return (d1 if r & 4 else 0) + (d2 if r & 2 else 0) + (d3 if r & 1 else 0)


def dim_of(p, r):
    return ORDERS[p][0 if r & 4 else 1 if r & 2 else 2]


def kernel(
    y_hbm, vc_hbm, vt_hbm, lc_ref, lt_ref, out_hbm,
    y, vc, vct, vt, acc, den, psend, precv, wown, qsend, qown, qrecv, q2send, q2recv, s, tbuf,
    in_sem, out_sem, p_ss, p_rs, c_ss, c_rs, q_ss, q_rs, s_ss, s_rs, d_ss, d_rs, t_ss, t_rs,
):
    c, t = lax.axis_index("cmp"), lax.axis_index("tgt")
    rows, cols = y.shape[1], y.shape[2]
    kb = vc.shape[1] // 8
    kcs = kb // CHUNKS
    tb = vt.shape[1] // 16

    cmp_peer = {d: {"cmp": cmp_at(c, d), "tgt": t} for d in (1, 2, 4)}
    tgt_peer = {k: {"cmp": c, "tgt": tgt_at(t, k)} for k in range(1, 9)}

    def remote(src, dst, ss, rs, peer):
        return pltpu.make_async_remote_copy(
            src_ref=src, dst_ref=dst, send_sem=ss, recv_sem=rs, device_id=peer, device_id_type=MESH
        )

    barrier = pltpu.get_barrier_semaphore()
    for peer in list(cmp_peer.values()) + list(tgt_peer.values()):
        pl.semaphore_signal(barrier, inc=1, device_id=peer, device_id_type=MESH)

    vc_in = [
        pltpu.make_async_copy(
            vc_hbm.at[:, pl.ds(pl.multiple_of(cmp_at(c, j) * kb, kb), kb)],
            vc.at[:, pl.ds(j * kb, kb)],
            in_sem.at[j],
        )
        for j in range(8)
    ]
    y_in = [
        pltpu.make_async_copy(y_hbm.at[:, pl.ds(p * cols, cols)], y.at[p], in_sem.at[8 + p])
        for p in range(PARTS)
    ]
    vt_in = [
        pltpu.make_async_copy(
            vt_hbm.at[:, pl.ds(pl.multiple_of(tgt_at(t, k) * tb, tb), tb)],
            vt.at[:, pl.ds(k * tb, tb)],
            in_sem.at[11 + k],
        )
        for k in range(16)
    ]
    y_in[0].start()
    for j in (7, 3, 5, 1):
        vc_in[j].start()
    y_in[1].start()
    y_in[2].start()
    for j in (6, 2, 4, 0):
        vc_in[j].start()
    for copy in vt_in:
        copy.start()

    def transpose(j):
        vc_in[j].wait()
        vct[pl.ds(j * kb, kb), :] = vc[:, pl.ds(j * kb, kb)].T

    def product(h, p, rs):
        lhs = [vct[pl.ds(block_of(p, r) * kb + h * kcs, kcs), :] for r in rs]
        return jnp.dot(jnp.concatenate(lhs, axis=0), y[p], preferred_element_type=F32)

    def p_copy(h, p, r):
        return remote(
            psend.at[h, p, r - 1], precv.at[h, p, r - 1], p_ss.at[h, p, r - 1], p_rs.at[h, p, r - 1],
            cmp_peer[dim_of(p, r)],
        )

    def got(h, p, r):
        p_copy(h, p, r).wait_recv()
        return precv[h, p, r - 1].astype(F32)

    def p1_compute(h, p):
        prod = product(h, p, (7, 6, 5, 4))
        for i, r in enumerate((7, 6, 5, 4)):
            psend[h, p, r - 1] = prod[i * kcs : (i + 1) * kcs].astype(BF16)

    def p1_send(h, p, rs=(7, 6, 5, 4)):
        for r in rs:
            p_copy(h, p, r).start()

    def p2(h, p):
        prod = product(h, p, (3, 2))
        for i, r in enumerate((3, 2)):
            psend[h, p, r - 1] = (prod[i * kcs : (i + 1) * kcs] + got(h, p, r + 4)).astype(BF16)
            p_copy(h, p, r).start()

    def p3(h, p):
        prod = product(h, p, (1, 0))
        wown[h, p] = prod[kcs:]
        psend[h, p, 0] = (prod[:kcs] + got(h, p, 5) + got(h, p, 3)).astype(BF16)
        p_copy(h, p, 1).start()

    def c_copy(h):
        return remote(qsend.at[h], qrecv.at[h], c_ss.at[h], c_rs.at[h], tgt_peer[8])

    def pf(h):
        w = jnp.concatenate(
            [wown[h, p] + got(h, p, 4) + got(h, p, 2) + got(h, p, 1) for p in range(PARTS)], axis=1
        )
        high = w.astype(BF16)
        low = (w - high.astype(F32)).astype(BF16)
        both = jnp.concatenate([high, low], axis=0)
        for k in list(range(8, 16)) + list(range(8)):
            if k % 2:
                continue
            q = jnp.dot(both, vt[:, k * tb : (k + 2) * tb], preferred_element_type=F32)
            q = q[:kcs] + q[kcs:]
            for i in range(2):
                block = q[:, i * tb : (i + 1) * tb]
                if k >= 8:
                    qsend[h, k - 8 + i] = block
                else:
                    qown[h, k + i] = block
            if k == 14:
                c_copy(h).start()

    def q_copy(h, k):
        return remote(q2send.at[h, k - 1], q2recv.at[h, k - 1], q_ss.at[h, k - 1], q_rs.at[h, k - 1], tgt_peer[k])

    def m1(h):
        c_copy(h).wait_recv()
        for k in (3, 7, 1, 2, 5, 6, 4):
            q2send[h, k - 1] = qown[h, k] + qrecv[h, k]
            q_copy(h, k).start()

    def s_copy(h, k):
        return remote(s.at[h, 0, 0], s.at[h, 0, k], s_ss.at[h, k - 1], s_rs.at[h, k - 1], tgt_peer[k])

    def m2(h):
        total = qown[h, 0] + qrecv[h, 0]
        for k in range(1, 8):
            q_copy(h, k).wait_recv()
            total += q2recv[h, k - 1]
        s[h, 0, 0] = (total / den[h * kcs : (h + 1) * kcs, :]).astype(BF16)
        for k in (3, 7, 1, 2, 5, 6, 4):
            s_copy(h, k).start()

    def d_copy(h):
        return remote(s.at[h, 0], s.at[h, 1], d_ss.at[h], d_rs.at[h], tgt_peer[8])

    def m3(h):
        for k in range(1, 8):
            s_copy(h, k).wait_recv()
        d_copy(h).start()

    def t_copy(h, p, r):
        d = 4 if r & 4 else 2 if r & 2 else 1
        return remote(
            tbuf.at[h, p, r - d], tbuf.at[h, p, r], t_ss.at[h, p, r - 1], t_rs.at[h, p, r - 1],
            cmp_peer[dim_of(p, r)],
        )

    def m4(h):
        d_copy(h).wait_recv()
        lhs = jnp.concatenate([s[h, i, k] for i in range(2) for k in range(8)], axis=1)
        for p in range(PARTS):
            part = lax.dot_general(
                lhs, vt[p * cols : (p + 1) * cols, :], (((1,), (1,)), ((), ())), preferred_element_type=F32
            )
            tbuf[h, p, 0] = part.astype(BF16)
            for r in (4, 2, 1):
                t_copy(h, p, r).start()

    def a1(h):
        for p in range(PARTS):
            t_copy(h, p, 1).wait_recv()
            t_copy(h, p, 3).start()
            t_copy(h, p, 5).start()
            t_copy(h, p, 2).wait_recv()
            t_copy(h, p, 6).start()

    def a2(h):
        for p in range(PARTS):
            t_copy(h, p, 3).wait_recv()
            t_copy(h, p, 7).start()

    def o_copy(p, i):
        start = pl.multiple_of(i * ROW_TILE, ROW_TILE)
        return pltpu.make_async_copy(
            acc.at[p, pl.ds(start, ROW_TILE)],
            out_hbm.at[pl.ds(start, ROW_TILE), pl.ds(p * cols, cols)],
            out_sem.at[p, i],
        )

    def accumulate(h, group, first, last):
        for p in range(PARTS):
            for r in group:
                if r in (4, 5, 6, 7):
                    t_copy(h, p, r).wait_recv()
            rhs = jnp.concatenate([tbuf[h, p, r] for r in group], axis=0)

            @pl.loop(0, rows // ROW_TILE)
            def _(i):
                at = pl.ds(pl.multiple_of(i * ROW_TILE, ROW_TILE), ROW_TILE)
                lhs = jnp.concatenate(
                    [vc[at, pl.ds(block_of(p, r) * kb + h * kcs, kcs)] for r in group], axis=1
                )
                prod = jnp.dot(lhs, rhs, preferred_element_type=F32)
                acc[p, at, :] = prod if first else acc[p, at, :] + prod
                if last:
                    o_copy(p, i).start()

    y_in[0].wait()
    for j in (7, 3, 5, 1):
        transpose(j)
    p1_compute(0, 0)
    pl.semaphore_wait(barrier, len(cmp_peer) + len(tgt_peer))
    p1_send(0, 0)
    transpose(6)
    transpose(2)
    y_in[1].wait()
    p1_compute(0, 1)
    p1_send(0, 1)
    transpose(4)
    y_in[2].wait()
    p1_compute(0, 2)
    p1_send(0, 2)
    transpose(0)
    den[...] = (
        jnp.broadcast_to(lc_ref[...], (tb, kb)).T * jnp.broadcast_to(lt_ref[...], (kb, tb)) + 0.25
    )
    for copy in vt_in:
        copy.wait()

    for p in range(PARTS):
        p1_compute(1, p)
    for p in range(PARTS):
        p2(0, p)
    for p in range(PARTS):
        p1_send(1, p, (7, 6))
    for p in range(PARTS):
        p3(0, p)
    for p in range(PARTS):
        p1_send(1, p, (5, 4))
    pf(0)
    for p in range(PARTS):
        p2(1, p)
    m1(0)
    for p in range(PARTS):
        p3(1, p)
    m2(0)
    pf(1)
    m3(0)
    m1(1)
    m4(0)
    m2(1)
    a1(0)
    m3(1)
    a2(0)
    m4(1)
    accumulate(0, (0, 1, 2, 4), True, False)
    a1(1)
    a2(1)
    accumulate(0, (3, 5, 6, 7), False, False)
    accumulate(1, (0, 1, 2, 4), False, False)
    accumulate(1, (3, 5, 6, 7), False, True)

    for h in range(CHUNKS):
        c_copy(h).wait_send()
        d_copy(h).wait_send()
        for r in range(1, 8):
            q_copy(h, r).wait_send()
            s_copy(h, r).wait_send()
            for p in range(PARTS):
                p_copy(h, p, r).wait_send()
                t_copy(h, p, r).wait_send()
    for p in range(PARTS):
        for i in range(rows // ROW_TILE):
            o_copy(p, i).wait()


def shards(affinity, comp_vectors, targ_vectors, comp_values, targ_values):
    rows, targets = affinity.shape
    kc, kt = comp_vectors.shape[1], targ_vectors.shape[1]
    cols, kb, tb = targets // PARTS, kc // 8, kt // 16
    n, kcs = CHUNKS, kb // CHUNKS
    any_space = pl.BlockSpec(memory_space=pl.ANY)
    vmem = pl.BlockSpec(memory_space=pltpu.VMEM)
    dma = pltpu.SemaphoreType.DMA
    return pl.pallas_call(
        kernel,
        out_shape=jax.ShapeDtypeStruct((rows, targets), F32),
        in_specs=[any_space, any_space, any_space, vmem, vmem],
        out_specs=any_space,
        scratch_shapes=[
            pltpu.VMEM((PARTS, rows, cols), BF16),
            pltpu.VMEM((rows, kc), BF16),
            pltpu.VMEM((kc, rows), BF16),
            pltpu.VMEM((targets, kt), BF16),
            pltpu.VMEM((PARTS, rows, cols), F32),
            pltpu.VMEM((kb, tb), F32),
            pltpu.VMEM((n, PARTS, 7, kcs, cols), BF16),
            pltpu.VMEM((n, PARTS, 7, kcs, cols), BF16),
            pltpu.VMEM((n, PARTS, kcs, cols), F32),
            pltpu.VMEM((n, 8, kcs, tb), F32),
            pltpu.VMEM((n, 8, kcs, tb), F32),
            pltpu.VMEM((n, 8, kcs, tb), F32),
            pltpu.VMEM((n, 7, kcs, tb), F32),
            pltpu.VMEM((n, 7, kcs, tb), F32),
            pltpu.VMEM((n, 2, 8, kcs, tb), BF16),
            pltpu.VMEM((n, PARTS, 8, kcs, cols), BF16),
            dma((27,)),
            dma((PARTS, rows // ROW_TILE)),
            dma((n, PARTS, 7)),
            dma((n, PARTS, 7)),
            dma((n,)),
            dma((n,)),
            dma((n, 7)),
            dma((n, 7)),
            dma((n, 7)),
            dma((n, 7)),
            dma((n,)),
            dma((n,)),
            dma((n, PARTS, 7)),
            dma((n, PARTS, 7)),
        ],
        compiler_params=pltpu.CompilerParams(
            collective_id=0, has_side_effects=True, vmem_limit_bytes=60 << 20
        ),
    )(affinity, comp_vectors, targ_vectors, comp_values[None, :], targ_values[None, :])


def solution(mesh):
    in_specs = (P("cmp", "tgt"), P("cmp", None), P("tgt", None), P("cmp"), P("tgt"))
    out_specs = P("cmp", "tgt")
    return jax.shard_map(shards, mesh=mesh, in_specs=in_specs, out_specs=out_specs, check_vma=False)
```

```python
import functools

import jax
import jax.numpy as jnp
from jax import lax
from jax.experimental import pallas as pl
from jax.experimental.pallas import tpu as pltpu
from jax.sharding import PartitionSpec as P

MESH = pl.DeviceIdType.MESH
F32, BF16 = jnp.float32, jnp.bfloat16
CHUNKS = 4
PARTS = 3
SUM_DIMS = ((1, 2, 4), (2, 1, 4), (4, 1, 2))
GATHER_DIMS = ((1, 2, 4), (2, 1, 4), (4, 2, 1))
ROW_TILE = 512
STEPS = (
    ("ps", 0, 2), ("tr", 6), ("tr", 5), ("tr", 2), ("ps", 0, 0), ("ps", 0, 1), ("pt", 0, 0), ("pc", 1, 0),
    ("ps", 1, 0), ("pt", 0, 1), ("pc", 1, 1), ("pc", 1, 2), ("ps", 1, 1), ("ps", 1, 2), ("tr", 3), ("tr", 0),
    ("pt", 1, 2), ("p2", 0, 1), ("p2", 0, 0), ("tr", 1), ("tr", 4), ("tr", 7), ("pt", 1, 0), ("pt", 0, 2),
    ("p2", 0, 2), ("pc", 3, 1), ("p2", 1, 0), ("pc", 2, 0), ("pt", 1, 1), ("p3", 0, 0), ("p3", 0, 1), ("p2", 1, 1),
    ("p2", 1, 2), ("setup",), ("p3", 0, 2), ("pc", 3, 0), ("p3", 1, 0), ("ps", 3, 0), ("pt", 3, 0), ("ps", 3, 1),
    ("p3", 1, 1), ("pc", 2, 1), ("ps", 2, 0), ("pc", 3, 2), ("ps", 3, 2), ("pt", 3, 2), ("p3", 1, 2), ("ps", 2, 1),
    ("pf", 0), ("p2", 3, 0), ("pt", 2, 0), ("pc", 2, 2), ("ps", 2, 2), ("pt", 3, 1), ("m1", 0), ("p2", 3, 1),
    ("pf", 1), ("p2", 2, 0), ("p2", 3, 2), ("pt", 2, 2), ("pt", 2, 1), ("m1", 1), ("p2", 2, 1), ("p3", 3, 0),
    ("p3", 3, 1), ("m2", 0), ("p2", 2, 2), ("p3", 2, 0), ("p3", 3, 2), ("p3", 2, 1), ("m2", 1), ("m3", 0),
    ("p3", 2, 2), ("pf", 3), ("m3", 1), ("m1", 3), ("m5", 0), ("pf", 2), ("m6", 0), ("m5", 1), ("m1", 2), ("m2", 3),
    ("m6", 1), ("m2", 2), ("a1", 0, 0), ("a1", 0, 1), ("m3", 3), ("a1", 1, 0), ("m3", 2), ("a1", 0, 2), ("a1", 1, 1),
    ("acc", 0, 0, 1), ("m5", 3), ("a1", 1, 2), ("a2", 0, 0), ("a2", 0, 1), ("a2", 1, 0), ("acc", 0, 0, 0),
    ("a2", 1, 1), ("m6", 3), ("m5", 2), ("acc", 0, 0, 2), ("m6", 2), ("a2", 1, 2), ("a1", 3, 0), ("a2", 0, 2),
    ("a1", 3, 2), ("acc", 0, 1, 0), ("acc", 0, 1, 1), ("a1", 2, 0), ("a1", 2, 2), ("a1", 3, 1), ("a1", 2, 1),
    ("acc", 1, 0, 1), ("acc", 1, 0, 2), ("a2", 3, 0), ("a2", 3, 2), ("a2", 2, 0), ("a2", 2, 2), ("a2", 3, 1),
    ("acc", 1, 0, 0), ("a2", 2, 1), ("acc", 0, 1, 2), ("acc", 1, 1, 0), ("acc", 1, 1, 2), ("acc", 1, 1, 1),)


def flip4(v, bits):
    return (v, v + 1 - 2 * lax.rem(v, 2), 3 - v, lax.rem(v + 2, 4))[bits]


def cmp_at(c, j):
    y = lax.rem(c, 4)
    base = c - y
    return (4 - base if j & 4 else base) + flip4(y, j & 3)


def tgt_at(t, k):
    x, z, core = t // 4, lax.rem(t // 2, 2), lax.rem(t, 2)
    z = 1 - z if k & 4 else z
    core = 1 - core if k & 8 else core
    return flip4(x, k & 3) * 4 + z * 2 + core


def block_of(dims, r):
    return (dims[0] if r & 4 else 0) + (dims[1] if r & 2 else 0) + (dims[2] if r & 1 else 0)


def dim_of(dims, r):
    return dims[0 if r & 4 else 1 if r & 2 else 2]


def kernel(
    y_hbm, vc_hbm, vt_hbm, lc_ref, lt_ref, out_hbm,
    y, vc, vct, vt, vtt, acc, den, psend, precv, wown, qsend, qown, qrecv, q2send, q2recv, s, tbuf,
    in_sem, out_sem, p_ss, p_rs, c_ss, c_rs, q_ss, q_rs, s_ss, s_rs, d_ss, d_rs, t_ss, t_rs,
):
    c, t = lax.axis_index("cmp"), lax.axis_index("tgt")
    rows, cols = y.shape[1], y.shape[2]
    kb = vc.shape[1] // 8
    kcs = kb // CHUNKS
    half = kb // 2
    tb = vt.shape[1] // 16

    cmp_peer = {d: {"cmp": cmp_at(c, d), "tgt": t} for d in (1, 2, 4)}
    tgt_peer = {k: {"cmp": c, "tgt": tgt_at(t, k)} for k in range(1, 9)}

    def remote(src, dst, ss, rs, peer):
        return pltpu.make_async_remote_copy(
            src_ref=src, dst_ref=dst, send_sem=ss, recv_sem=rs, device_id=peer, device_id_type=MESH
        )

    barrier = pltpu.get_barrier_semaphore()
    for peer in list(cmp_peer.values()) + list(tgt_peer.values()):
        pl.semaphore_signal(barrier, inc=1, device_id=peer, device_id_type=MESH)

    vc_in = {}
    for i in range(2):
        for j in range(8):
            vc_in[i, j] = pltpu.make_async_copy(
                vc_hbm.at[:, pl.ds(pl.multiple_of(cmp_at(c, j) * kb + i * half, half), half)],
                vc.at[:, pl.ds(j * kb + i * half, half)],
                in_sem.at[i * 8 + j],
            )
    y_in = [
        pltpu.make_async_copy(y_hbm.at[:, pl.ds(p * cols, cols)], y.at[p], in_sem.at[16 + p])
        for p in range(PARTS)
    ]
    vt_in = [
        pltpu.make_async_copy(
            vt_hbm.at[:, pl.ds(pl.multiple_of(tgt_at(t, k) * tb, tb), tb)],
            vt.at[:, pl.ds(k * tb, tb)],
            in_sem.at[19 + k],
        )
        for k in range(16)
    ]
    load_order = (7, 3, 5, 1, 6, 2, 4, 0)
    for j in load_order[:4]:
        vc_in[0, j].start()
    y_in[0].start()
    for j in load_order[4:]:
        vc_in[0, j].start()
    y_in[1].start()
    y_in[2].start()
    for j in load_order:
        vc_in[1, j].start()
    for copy in vt_in:
        copy.start()

    def transpose(i, js):
        for j in js:
            vc_in[i, j].wait()
            at = pl.ds(j * kb + i * half, half)
            vct[at, :] = vc[:, at].T

    def p_copy(h, p, r):
        return remote(
            psend.at[h, p, r - 1], precv.at[h, p, r - 1], p_ss.at[h, p, r - 1], p_rs.at[h, p, r - 1],
            cmp_peer[dim_of(SUM_DIMS[p], r)],
        )

    def got(h, p, r):
        p_copy(h, p, r).wait_recv()
        return precv[h, p, r - 1].astype(F32)

    def pc(h, p):
        lhs = [
            vct[pl.ds(block_of(SUM_DIMS[p], r) * kb + h * kcs, kcs), :] for r in range(7, -1, -1)
        ]
        prod = jnp.dot(jnp.concatenate(lhs, axis=0), y[p], preferred_element_type=F32)
        for i, r in enumerate(range(7, -1, -1)):
            block = prod[i * kcs : (i + 1) * kcs]
            if r >= 4:
                psend[h, p, r - 1] = block.astype(BF16)
            else:
                wown[h, p, r] = block

    def ps(h, p):
        p_copy(h, p, 7).start()
        p_copy(h, p, 6).start()

    def pt(h, p):
        p_copy(h, p, 5).start()
        p_copy(h, p, 4).start()

    def p2(h, p):
        for r in (3, 2):
            psend[h, p, r - 1] = (wown[h, p, r] + got(h, p, r + 4)).astype(BF16)
            p_copy(h, p, r).start()

    def p3(h, p):
        psend[h, p, 0] = (wown[h, p, 1] + got(h, p, 5) + got(h, p, 3)).astype(BF16)
        p_copy(h, p, 1).start()

    def c_copy(h):
        return remote(qsend.at[h], qrecv.at[h], c_ss.at[h], c_rs.at[h], tgt_peer[8])

    def pf(h):
        w = jnp.concatenate(
            [wown[h, p, 0] + got(h, p, 4) + got(h, p, 2) + got(h, p, 1) for p in range(PARTS)], axis=1
        )
        high = w.astype(BF16)
        low = (w - high.astype(F32)).astype(BF16)
        both = jnp.concatenate([high, low], axis=0)
        for k in (8, 10, 12, 14, 0, 2, 4, 6):
            q = jnp.dot(both, vt[:, k * tb : (k + 2) * tb], preferred_element_type=F32)
            q = q[:kcs] + q[kcs:]
            for i in range(2):
                block = q[:, i * tb : (i + 1) * tb]
                if k >= 8:
                    qsend[h, k - 8 + i] = block
                else:
                    qown[h, k + i] = block
            if k == 14:
                c_copy(h).start()

    def q_copy(h, k):
        if k == 4:
            return remote(q2send.at[h, 3], q2recv.at[h, 3], q_ss.at[h, 3], q_rs.at[h, 3], tgt_peer[4])
        return remote(q2send.at[h, k - 1], q2recv.at[h, k - 1], q_ss.at[h, k - 1], q_rs.at[h, k - 1], tgt_peer[k & 3])

    def m1(h):
        c_copy(h).wait_recv()
        for k in (7, 3, 5, 6, 1, 2):
            q2send[h, k - 1] = qown[h, k] + qrecv[h, k]
            q_copy(h, k).start()

    def m2(h):
        total = qown[h, 4] + qrecv[h, 4]
        for k in (5, 6, 7):
            q_copy(h, k).wait_recv()
            total += q2recv[h, k - 1]
        q2send[h, 3] = total
        q_copy(h, 4).start()
        total = qown[h, 0] + qrecv[h, 0]
        for k in (1, 2, 3):
            q_copy(h, k).wait_recv()
            total += q2recv[h, k - 1]
        qown[h, 0] = total

    def s_copy(h, k):
        return remote(s.at[h, 0, 0], s.at[h, 0, k], s_ss.at[h, k - 1], s_rs.at[h, k - 1], tgt_peer[k])

    def m3(h):
        q_copy(h, 4).wait_recv()
        total = qown[h, 0] + q2recv[h, 3]
        s[h, 0, 0] = (total / den[h * kcs : (h + 1) * kcs, :]).astype(BF16)
        for k in (7, 3, 5, 6, 1, 2, 4):
            s_copy(h, k).start()

    def d_copy(h):
        return remote(s.at[h, 0], s.at[h, 1], d_ss.at[h], d_rs.at[h], tgt_peer[8])

    def m5(h):
        for k in range(1, 8):
            s_copy(h, k).wait_recv()
        d_copy(h).start()

    def t_copy(h, p, r):
        d = 4 if r & 4 else 2 if r & 2 else 1
        return remote(
            tbuf.at[h, p, r - d], tbuf.at[h, p, r], t_ss.at[h, p, r - 1], t_rs.at[h, p, r - 1],
            cmp_peer[dim_of(GATHER_DIMS[p], r)],
        )

    def m6(h):
        d_copy(h).wait_recv()
        lhs = jnp.concatenate([s[h, i, k] for i in range(2) for k in range(8)], axis=1)
        part = jnp.dot(lhs, vtt[...], preferred_element_type=F32).astype(BF16)
        for p in range(PARTS):
            tbuf[h, p, 0] = part[:, p * cols : (p + 1) * cols]
        for r in (1, 2, 4):
            for p in range(PARTS):
                t_copy(h, p, r).start()

    def a1(h, p):
        t_copy(h, p, 1).wait_recv()
        t_copy(h, p, 2).wait_recv()
        for r in (3, 5, 6):
            t_copy(h, p, r).start()

    def a2(h, p):
        t_copy(h, p, 3).wait_recv()
        t_copy(h, p, 7).start()

    def o_copy(p, i):
        start = pl.multiple_of(i * ROW_TILE, ROW_TILE)
        return pltpu.make_async_copy(
            acc.at[p, pl.ds(start, ROW_TILE)],
            out_hbm.at[pl.ds(start, ROW_TILE), pl.ds(p * cols, cols)],
            out_sem.at[p, i],
        )

    per_half = CHUNKS // 2

    def acc_step(i, far, p):
        chunks = range(i * per_half, (i + 1) * per_half)
        group = (3, 5, 6, 7) if far else (0, 1, 2, 4)
        first, last = not (i or far), i and far
        for h in chunks:
            for r in group:
                if r >= 4:
                    t_copy(h, p, r).wait_recv()
        rhs = jnp.concatenate([tbuf[h, p, r] for r in group for h in chunks], axis=0)

        @pl.loop(0, rows // ROW_TILE)
        def _(n):
            at = pl.ds(pl.multiple_of(n * ROW_TILE, ROW_TILE), ROW_TILE)
            lhs = jnp.concatenate(
                [vc[at, pl.ds(block_of(GATHER_DIMS[p], r) * kb + i * half, half)] for r in group], axis=1
            )
            prod = jnp.dot(lhs, rhs, preferred_element_type=F32)
            acc[p, at, :] = prod if first else acc[p, at, :] + prod
            if last:
                o_copy(p, n).start()

    def setup():
        den[...] = (
            jnp.broadcast_to(lc_ref[...], (tb, kb)).T * jnp.broadcast_to(lt_ref[...], (kb, tb)) + 0.25
        )
        for copy in vt_in:
            copy.wait()
        vtt[...] = vt[...].T

    transpose(0, load_order)
    for p in range(PARTS):
        y_in[p].wait()
        pc(0, p)
    pl.semaphore_wait(barrier, len(cmp_peer) + len(tgt_peer))

    steps = {
        "tr": lambda n: transpose(1, (load_order[n],)), "setup": setup, "pc": pc, "ps": ps, "pt": pt,
        "p2": p2, "p3": p3, "pf": pf, "m1": m1, "m2": m2, "m3": m3, "m5": m5, "m6": m6, "a1": a1,
        "a2": a2, "acc": acc_step,
    }
    for name, *where in STEPS:
        steps[name](*where)

    for h in range(CHUNKS):
        c_copy(h).wait_send()
        d_copy(h).wait_send()
        for r in range(1, 8):
            q_copy(h, r).wait_send()
            s_copy(h, r).wait_send()
            for p in range(PARTS):
                p_copy(h, p, r).wait_send()
                t_copy(h, p, r).wait_send()
    for p in range(PARTS):
        for i in range(rows // ROW_TILE):
            o_copy(p, i).wait()


def shards(affinity, comp_vectors, targ_vectors, comp_values, targ_values):
    rows, targets = affinity.shape
    kc, kt = comp_vectors.shape[1], targ_vectors.shape[1]
    cols, kb, tb = targets // PARTS, kc // 8, kt // 16
    n, kcs = CHUNKS, kb // CHUNKS
    any_space = pl.BlockSpec(memory_space=pl.ANY)
    vmem = pl.BlockSpec(memory_space=pltpu.VMEM)
    dma = pltpu.SemaphoreType.DMA
    return pl.pallas_call(
        kernel,
        out_shape=jax.ShapeDtypeStruct((rows, targets), F32),
        in_specs=[any_space, any_space, any_space, vmem, vmem],
        out_specs=any_space,
        scratch_shapes=[
            pltpu.VMEM((PARTS, rows, cols), BF16),
            pltpu.VMEM((rows, kc), BF16),
            pltpu.VMEM((kc, rows), BF16),
            pltpu.VMEM((targets, kt), BF16),
            pltpu.VMEM((kt, targets), BF16),
            pltpu.VMEM((PARTS, rows, cols), F32),
            pltpu.VMEM((kb, tb), F32),
            pltpu.VMEM((n, PARTS, 7, kcs, cols), BF16),
            pltpu.VMEM((n, PARTS, 7, kcs, cols), BF16),
            pltpu.VMEM((n, PARTS, 4, kcs, cols), F32),
            pltpu.VMEM((n, 8, kcs, tb), F32),
            pltpu.VMEM((n, 8, kcs, tb), F32),
            pltpu.VMEM((n, 8, kcs, tb), F32),
            pltpu.VMEM((n, 7, kcs, tb), F32),
            pltpu.VMEM((n, 7, kcs, tb), F32),
            pltpu.VMEM((n, 2, 8, kcs, tb), BF16),
            pltpu.VMEM((n, PARTS, 8, kcs, cols), BF16),
            dma((35,)),
            dma((PARTS, rows // ROW_TILE)),
            dma((n, PARTS, 7)),
            dma((n, PARTS, 7)),
            dma((n,)),
            dma((n,)),
            dma((n, 7)),
            dma((n, 7)),
            dma((n, 7)),
            dma((n, 7)),
            dma((n,)),
            dma((n,)),
            dma((n, PARTS, 7)),
            dma((n, PARTS, 7)),
        ],
        compiler_params=pltpu.CompilerParams(
            collective_id=0, has_side_effects=True, vmem_limit_bytes=60 << 20
        ),
    )(affinity, comp_vectors, targ_vectors, comp_values[None, :], targ_values[None, :])


def solution(mesh):
    in_specs = (P("cmp", "tgt"), P("cmp", None), P("tgt", None), P("cmp"), P("tgt"))
    out_specs = P("cmp", "tgt")
    return jax.shard_map(shards, mesh=mesh, in_specs=in_specs, out_specs=out_specs, check_vma=False)
```

```python
import functools

import jax
import jax.numpy as jnp
from jax import lax
from jax.experimental import pallas as pl
from jax.experimental.pallas import tpu as pltpu
from jax.sharding import PartitionSpec as P

MESH = pl.DeviceIdType.MESH
F32, BF16 = jnp.float32, jnp.bfloat16
CHUNKS = 4
PARTS = 3
SUM_DIMS = ((1, 2, 4), (2, 1, 4), (4, 1, 2))
GATHER_DIMS = ((1, 2, 4), (2, 1, 4), (4, 2, 1))
ROW_TILE = 512
LAST_TILE = 256
FAR = (3, 5, 6, 7)
STEPS = (
    ("ps", 0, 2), ("tr", 6), ("tr", 5), ("tr", 2), ("ps", 0, 0), ("ps", 0, 1), ("pt", 0, 0), ("pc", 1, 0),
    ("ps", 1, 0), ("pt", 0, 1), ("pc", 1, 1), ("pc", 1, 2), ("ps", 1, 1), ("ps", 1, 2), ("tr", 3), ("tr", 0),
    ("pt", 1, 2), ("p2", 0, 1), ("p2", 0, 0), ("tr", 1), ("tr", 4), ("tr", 7), ("pt", 1, 0), ("pt", 0, 2),
    ("p2", 0, 2), ("pc", 3, 1), ("p2", 1, 0), ("pc", 2, 0), ("pt", 1, 1), ("p3", 0, 0), ("p3", 0, 1), ("p2", 1, 1),
    ("p2", 1, 2), ("setup",), ("p3", 0, 2), ("pc", 3, 0), ("p3", 1, 0), ("ps", 3, 0), ("pt", 3, 0), ("ps", 3, 1),
    ("p3", 1, 1), ("pc", 2, 1), ("ps", 2, 0), ("pc", 3, 2), ("ps", 3, 2), ("pt", 3, 2), ("p3", 1, 2), ("ps", 2, 1),
    ("pf", 0), ("p2", 3, 0), ("pt", 2, 0), ("pc", 2, 2), ("ps", 2, 2), ("pt", 3, 1), ("m1", 0), ("p2", 3, 1),
    ("pf", 1), ("p2", 2, 0), ("p2", 3, 2), ("pt", 2, 2), ("pt", 2, 1), ("m1", 1), ("p2", 2, 1), ("p3", 3, 0),
    ("p3", 3, 1), ("m2", 0), ("p2", 2, 2), ("p3", 2, 0), ("p3", 3, 2), ("p3", 2, 1), ("m2", 1), ("m3", 0),
    ("p3", 2, 2), ("pf", 3), ("m3", 1), ("m1", 3), ("m5", 0), ("pf", 2), ("m6", 0), ("m5", 1), ("m1", 2), ("m2", 3),
    ("m6", 1), ("m2", 2), ("a1", 0, 0), ("a1", 0, 1), ("m3", 3), ("a1", 1, 0), ("m3", 2), ("a1", 0, 2), ("a1", 1, 1),
    ("acc", 0, 0, 1), ("m5", 3), ("a1", 1, 2), ("a2", 0, 0), ("a2", 0, 1), ("a2", 1, 0), ("acc", 0, 0, 0),
    ("a2", 1, 1), ("m6", 3), ("m5", 2), ("acc", 0, 0, 2), ("m6", 2), ("a2", 1, 2), ("a1", 3, 0), ("a2", 0, 2),
    ("a1", 3, 2), ("acc", 0, 1, 0), ("acc", 0, 1, 1), ("a1", 2, 0), ("a1", 2, 2), ("a1", 3, 1), ("a1", 2, 1),
    ("acc", 1, 0, 1), ("acc", 1, 0, 2), ("a2", 3, 0), ("a2", 3, 2), ("a2", 2, 0), ("a2", 2, 2), ("a2", 3, 1),
    ("acc", 1, 0, 0), ("a2", 2, 1), ("acc", 0, 1, 2), ("acc", 1, 1, 0), ("acc", 1, 1, 2), ("acc", 1, 1, 1),)


def flip4(v, bits):
    return (v, v + 1 - 2 * lax.rem(v, 2), 3 - v, lax.rem(v + 2, 4))[bits]


def cmp_at(c, j):
    y = lax.rem(c, 4)
    base = c - y
    return (4 - base if j & 4 else base) + flip4(y, j & 3)


def tgt_at(t, k):
    x, z, core = t // 4, lax.rem(t // 2, 2), lax.rem(t, 2)
    z = 1 - z if k & 4 else z
    core = 1 - core if k & 8 else core
    return flip4(x, k & 3) * 4 + z * 2 + core


def block_of(dims, r):
    return (dims[0] if r & 4 else 0) + (dims[1] if r & 2 else 0) + (dims[2] if r & 1 else 0)


def dim_of(dims, r):
    return dims[0 if r & 4 else 1 if r & 2 else 2]


def kernel(
    y_hbm, vc_hbm, vt_hbm, lc_ref, lt_ref, acc0, acc1, acc2, tfar, vcfar,
    y, vc, vct, vt, vtt, den, psend, precv, wown, qsend, qown, qrecv, q2send, q2recv, s, tbuf,
    in_sem, p_ss, p_rs, c_ss, c_rs, q_ss, q_rs, s_ss, s_rs, d_ss, d_rs, t_ss, t_rs,
):
    acc = (acc0, acc1, acc2)
    c, t = lax.axis_index("cmp"), lax.axis_index("tgt")
    rows, cols = y.shape[1], y.shape[2]
    kb = vc.shape[1] // 8
    kcs = kb // CHUNKS
    half = kb // 2
    tb = vt.shape[1] // 16

    cmp_peer = {d: {"cmp": cmp_at(c, d), "tgt": t} for d in (1, 2, 4)}
    tgt_peer = {k: {"cmp": c, "tgt": tgt_at(t, k)} for k in range(1, 9)}

    def remote(src, dst, ss, rs, peer):
        return pltpu.make_async_remote_copy(
            src_ref=src, dst_ref=dst, send_sem=ss, recv_sem=rs, device_id=peer, device_id_type=MESH
        )

    barrier = pltpu.get_barrier_semaphore()
    for peer in list(cmp_peer.values()) + list(tgt_peer.values()):
        pl.semaphore_signal(barrier, inc=1, device_id=peer, device_id_type=MESH)

    vc_in = {}
    for i in range(2):
        for j in range(8):
            vc_in[i, j] = pltpu.make_async_copy(
                vc_hbm.at[:, pl.ds(pl.multiple_of(cmp_at(c, j) * kb + i * half, half), half)],
                vc.at[:, pl.ds(j * kb + i * half, half)],
                in_sem.at[i * 8 + j],
            )
    y_in = [
        pltpu.make_async_copy(y_hbm.at[:, pl.ds(p * cols, cols)], y.at[p], in_sem.at[16 + p])
        for p in range(PARTS)
    ]
    vt_in = [
        pltpu.make_async_copy(
            vt_hbm.at[:, pl.ds(pl.multiple_of(tgt_at(t, k) * tb, tb), tb)],
            vt.at[:, pl.ds(k * tb, tb)],
            in_sem.at[19 + k],
        )
        for k in range(16)
    ]
    load_order = (7, 3, 5, 1, 6, 2, 4, 0)
    for j in load_order[:4]:
        vc_in[0, j].start()
    y_in[0].start()
    for j in load_order[4:]:
        vc_in[0, j].start()
    y_in[1].start()
    y_in[2].start()
    for j in load_order:
        vc_in[1, j].start()
    for copy in vt_in:
        copy.start()

    def transpose(i, js):
        for j in js:
            vc_in[i, j].wait()
            at = pl.ds(j * kb + i * half, half)
            vct[at, :] = vc[:, at].T

    def p_copy(h, p, r):
        return remote(
            psend.at[h, p, r - 1], precv.at[h, p, r - 1], p_ss.at[h, p, r - 1], p_rs.at[h, p, r - 1],
            cmp_peer[dim_of(SUM_DIMS[p], r)],
        )

    def got(h, p, r):
        p_copy(h, p, r).wait_recv()
        return precv[h, p, r - 1].astype(F32)

    def pc(h, p):
        lhs = [
            vct[pl.ds(block_of(SUM_DIMS[p], r) * kb + h * kcs, kcs), :] for r in range(7, -1, -1)
        ]
        prod = jnp.dot(jnp.concatenate(lhs, axis=0), y[p], preferred_element_type=F32)
        for i, r in enumerate(range(7, -1, -1)):
            block = prod[i * kcs : (i + 1) * kcs]
            if r >= 4:
                psend[h, p, r - 1] = block.astype(BF16)
            else:
                wown[h, p, r] = block

    def ps(h, p):
        p_copy(h, p, 7).start()
        p_copy(h, p, 6).start()

    def pt(h, p):
        p_copy(h, p, 5).start()
        p_copy(h, p, 4).start()

    def p2(h, p):
        for r in (3, 2):
            psend[h, p, r - 1] = (wown[h, p, r] + got(h, p, r + 4)).astype(BF16)
            p_copy(h, p, r).start()

    def p3(h, p):
        psend[h, p, 0] = (wown[h, p, 1] + got(h, p, 5) + got(h, p, 3)).astype(BF16)
        p_copy(h, p, 1).start()

    def c_copy(h):
        return remote(qsend.at[h], qrecv.at[h], c_ss.at[h], c_rs.at[h], tgt_peer[8])

    def pf(h):
        w = jnp.concatenate(
            [wown[h, p, 0] + got(h, p, 4) + got(h, p, 2) + got(h, p, 1) for p in range(PARTS)], axis=1
        )
        high = w.astype(BF16)
        low = (w - high.astype(F32)).astype(BF16)
        both = jnp.concatenate([high, low], axis=0)
        for k in (8, 10, 12, 14, 0, 2, 4, 6):
            q = jnp.dot(both, vt[:, k * tb : (k + 2) * tb], preferred_element_type=F32)
            q = q[:kcs] + q[kcs:]
            for i in range(2):
                block = q[:, i * tb : (i + 1) * tb]
                if k >= 8:
                    qsend[h, k - 8 + i] = block
                else:
                    qown[h, k + i] = block
            if k == 14:
                c_copy(h).start()

    def q_copy(h, k):
        if k == 4:
            return remote(q2send.at[h, 3], q2recv.at[h, 3], q_ss.at[h, 3], q_rs.at[h, 3], tgt_peer[4])
        return remote(q2send.at[h, k - 1], q2recv.at[h, k - 1], q_ss.at[h, k - 1], q_rs.at[h, k - 1], tgt_peer[k & 3])

    def m1(h):
        c_copy(h).wait_recv()
        for k in (7, 3, 5, 6, 1, 2):
            q2send[h, k - 1] = qown[h, k] + qrecv[h, k]
            q_copy(h, k).start()

    def m2(h):
        total = qown[h, 4] + qrecv[h, 4]
        for k in (5, 6, 7):
            q_copy(h, k).wait_recv()
            total += q2recv[h, k - 1]
        q2send[h, 3] = total
        q_copy(h, 4).start()
        total = qown[h, 0] + qrecv[h, 0]
        for k in (1, 2, 3):
            q_copy(h, k).wait_recv()
            total += q2recv[h, k - 1]
        qown[h, 0] = total

    def s_copy(h, k):
        return remote(s.at[h, 0, 0], s.at[h, 0, k], s_ss.at[h, k - 1], s_rs.at[h, k - 1], tgt_peer[k])

    def m3(h):
        q_copy(h, 4).wait_recv()
        total = qown[h, 0] + q2recv[h, 3]
        s[h, 0, 0] = (total / den[h * kcs : (h + 1) * kcs, :]).astype(BF16)
        for k in (7, 3, 5, 6, 1, 2, 4):
            s_copy(h, k).start()

    def d_copy(h):
        return remote(s.at[h, 0], s.at[h, 1], d_ss.at[h], d_rs.at[h], tgt_peer[8])

    def m5(h):
        for k in range(1, 8):
            s_copy(h, k).wait_recv()
        d_copy(h).start()

    def t_copy(h, p, r):
        d = 4 if r & 4 else 2 if r & 2 else 1
        return remote(
            tbuf.at[h, p, r - d], tbuf.at[h, p, r], t_ss.at[h, p, r - 1], t_rs.at[h, p, r - 1],
            cmp_peer[dim_of(GATHER_DIMS[p], r)],
        )

    def m6(h):
        d_copy(h).wait_recv()
        lhs = jnp.concatenate([s[h, i, k] for i in range(2) for k in range(8)], axis=1)
        part = jnp.dot(lhs, vtt[...], preferred_element_type=F32).astype(BF16)
        for p in range(PARTS):
            tbuf[h, p, 0] = part[:, p * cols : (p + 1) * cols]
        for r in (1, 2, 4):
            for p in range(PARTS):
                t_copy(h, p, r).start()

    def a1(h, p):
        t_copy(h, p, 1).wait_recv()
        t_copy(h, p, 2).wait_recv()
        for r in (3, 5, 6):
            t_copy(h, p, r).start()

    def a2(h, p):
        t_copy(h, p, 3).wait_recv()
        t_copy(h, p, 7).start()

    per_half = CHUNKS // 2

    def acc_step(i, far, p):
        chunks = range(i * per_half, (i + 1) * per_half)
        group = (3, 5, 6, 7) if far else (0, 1, 2, 4)
        for h in chunks:
            for r in group:
                if r >= 4:
                    t_copy(h, p, r).wait_recv()
        if i and far:
            for r in group:
                n = FAR.index(block_of(GATHER_DIMS[p], r))
                for h in chunks:
                    at = pl.ds(n * half + (h - chunks[0]) * kcs, kcs)
                    tfar[p, at, :] = tbuf[h, p, r]
            return
        first = not (i or far)
        rhs = jnp.concatenate([tbuf[h, p, r] for r in group for h in chunks], axis=0)

        @pl.loop(0, rows // ROW_TILE)
        def _(n):
            at = pl.ds(pl.multiple_of(n * ROW_TILE, ROW_TILE), ROW_TILE)
            lhs = jnp.concatenate(
                [vc[at, pl.ds(block_of(GATHER_DIMS[p], r) * kb + i * half, half)] for r in group], axis=1
            )
            prod = jnp.dot(lhs, rhs, preferred_element_type=F32)
            acc[p][at, :] = prod if first else acc[p][at, :] + prod

    def setup():
        den[...] = (
            jnp.broadcast_to(lc_ref[...], (tb, kb)).T * jnp.broadcast_to(lt_ref[...], (kb, tb)) + 0.25
        )
        for copy in vt_in:
            copy.wait()
        vtt[...] = vt[...].T
        for n, j in enumerate(FAR):
            vc_in_far = vc[:, pl.ds(j * kb + half, half)]
            vcfar[:, pl.ds(n * half, half)] = vc_in_far

    transpose(0, load_order)
    for p in range(PARTS):
        y_in[p].wait()
        pc(0, p)
    pl.semaphore_wait(barrier, len(cmp_peer) + len(tgt_peer))

    steps = {
        "tr": lambda n: transpose(1, (load_order[n],)), "setup": setup, "pc": pc, "ps": ps, "pt": pt,
        "p2": p2, "p3": p3, "pf": pf, "m1": m1, "m2": m2, "m3": m3, "m5": m5, "m6": m6, "a1": a1,
        "a2": a2, "acc": acc_step,
    }
    for name, *where in STEPS:
        steps[name](*where)

    for h in range(CHUNKS):
        c_copy(h).wait_send()
        d_copy(h).wait_send()
        for r in range(1, 8):
            q_copy(h, r).wait_send()
            s_copy(h, r).wait_send()
            for p in range(PARTS):
                p_copy(h, p, r).wait_send()
                t_copy(h, p, r).wait_send()


def finish(acc0, acc1, acc2, tfar, vcfar, out_hbm, buf, sem):
    acc = (acc0, acc1, acc2)
    rows, cols = acc0.shape
    copies = []
    for n in range(rows // LAST_TILE):
        at = pl.ds(n * LAST_TILE, LAST_TILE)
        for p in range(PARTS):
            prod = jnp.dot(vcfar[at, :], tfar[p], preferred_element_type=F32)
            buf[at, pl.ds(p * cols, cols)] = acc[p][at, :] + prod
        copy = pltpu.make_async_copy(buf.at[at], out_hbm.at[at], sem.at[n])
        copy.start()
        copies.append(copy)
    for copy in copies:
        copy.wait()


def shards(affinity, comp_vectors, targ_vectors, comp_values, targ_values):
    rows, targets = affinity.shape
    kc, kt = comp_vectors.shape[1], targ_vectors.shape[1]
    cols, kb, tb = targets // PARTS, kc // 8, kt // 16
    n, kcs = CHUNKS, kb // CHUNKS
    any_space = pl.BlockSpec(memory_space=pl.ANY)
    vmem = pl.BlockSpec(memory_space=pltpu.VMEM)
    dma = pltpu.SemaphoreType.DMA
    partial = pl.pallas_call(
        kernel,
        out_shape=[
            *[jax.ShapeDtypeStruct((rows, cols), F32)] * PARTS,
            jax.ShapeDtypeStruct((PARTS, 2 * kb, cols), BF16),
            jax.ShapeDtypeStruct((rows, 2 * kb), BF16),
        ],
        in_specs=[any_space, any_space, any_space, vmem, vmem],
        out_specs=[vmem] * (PARTS + 2),
        scratch_shapes=[
            pltpu.VMEM((PARTS, rows, cols), BF16),
            pltpu.VMEM((rows, kc), BF16),
            pltpu.VMEM((kc, rows), BF16),
            pltpu.VMEM((targets, kt), BF16),
            pltpu.VMEM((kt, targets), BF16),
            pltpu.VMEM((kb, tb), F32),
            pltpu.VMEM((n, PARTS, 7, kcs, cols), BF16),
            pltpu.VMEM((n, PARTS, 7, kcs, cols), BF16),
            pltpu.VMEM((n, PARTS, 4, kcs, cols), F32),
            pltpu.VMEM((n, 8, kcs, tb), F32),
            pltpu.VMEM((n, 8, kcs, tb), F32),
            pltpu.VMEM((n, 8, kcs, tb), F32),
            pltpu.VMEM((n, 7, kcs, tb), F32),
            pltpu.VMEM((n, 7, kcs, tb), F32),
            pltpu.VMEM((n, 2, 8, kcs, tb), BF16),
            pltpu.VMEM((n, PARTS, 8, kcs, cols), BF16),
            dma((35,)),
            dma((n, PARTS, 7)),
            dma((n, PARTS, 7)),
            dma((n,)),
            dma((n,)),
            dma((n, 7)),
            dma((n, 7)),
            dma((n, 7)),
            dma((n, 7)),
            dma((n,)),
            dma((n,)),
            dma((n, PARTS, 7)),
            dma((n, PARTS, 7)),
        ],
        compiler_params=pltpu.CompilerParams(
            collective_id=0, has_side_effects=True, vmem_limit_bytes=45 << 20
        ),
    )(affinity, comp_vectors, targ_vectors, comp_values[None, :], targ_values[None, :])
    return pl.pallas_call(
        finish,
        out_shape=jax.ShapeDtypeStruct((rows, targets), F32),
        in_specs=[vmem] * (PARTS + 2),
        out_specs=any_space,
        scratch_shapes=[pltpu.VMEM((rows, targets), F32), dma((rows // LAST_TILE,))],
        compiler_params=pltpu.CompilerParams(vmem_limit_bytes=8 << 20),
    )(*partial)


def solution(mesh):
    in_specs = (P("cmp", "tgt"), P("cmp", None), P("tgt", None), P("cmp"), P("tgt"))
    out_specs = P("cmp", "tgt")
    return jax.shard_map(shards, mesh=mesh, in_specs=in_specs, out_specs=out_specs, check_vma=False)
```

```python
import functools

import jax
import jax.numpy as jnp
from jax import lax
from jax.experimental import pallas as pl
from jax.experimental.pallas import tpu as pltpu
from jax.sharding import PartitionSpec as P

MESH = pl.DeviceIdType.MESH
F32, BF16 = jnp.float32, jnp.bfloat16
CHUNKS = 4
PARTS = 3
SUM_DIMS = ((1, 2, 4), (2, 1, 4), (4, 1, 2))
GATHER_DIMS = ((1, 2, 4), (2, 1, 4), (4, 2, 1))
ROW_TILE = 512
LAST_TILE = 256
FAR = (3, 5, 6, 7)
STEPS = (
    ("ps", 0, 1), ("pc", 1, 1), ("ps", 0, 0), ("tr", 7), ("pt", 0, 0), ("ps", 1, 1), ("tr", 2), ("tr", 0),
    ("pt", 1, 1), ("tr", 4), ("ps", 0, 2), ("tr", 3), ("tr", 6), ("pc", 1, 2), ("ps", 1, 2), ("p2", 0, 1),
    ("pc", 1, 0), ("p2", 0, 0), ("pt", 0, 2), ("tr", 5), ("ps", 1, 0), ("tr", 1), ("pc", 3, 1), ("p2", 0, 2),
    ("pt", 0, 1), ("pc", 3, 0), ("pt", 1, 2), ("ps", 3, 1), ("ps", 3, 0), ("pc", 2, 2), ("ps", 2, 2), ("p2", 1, 1),
    ("p3", 0, 0), ("pt", 1, 0), ("pc", 2, 1), ("p2", 1, 0), ("p3", 0, 1), ("p2", 1, 2), ("pc", 3, 2), ("p3", 0, 2),
    ("pc", 2, 0), ("ps", 3, 2), ("ps", 2, 0), ("pt", 3, 1), ("p3", 1, 1), ("pt", 3, 0), ("p3", 1, 0), ("p2", 3, 1),
    ("setup",), ("p3", 1, 2), ("ps", 2, 1), ("pf", 0), ("pt", 2, 0), ("pt", 3, 2), ("pt", 2, 2), ("p2", 3, 0),
    ("p2", 3, 2), ("p2", 2, 2), ("m1", 0), ("p3", 3, 1), ("p2", 2, 0), ("pf", 1), ("pt", 2, 1), ("p3", 3, 0),
    ("p2", 2, 1), ("p3", 3, 2), ("m1", 1), ("m2", 0), ("p3", 2, 0), ("p3", 2, 1), ("p3", 2, 2), ("pf", 3), ("m3", 0),
    ("m2", 1), ("m1", 3), ("pf", 2), ("m3", 1), ("m5", 0), ("m1", 2), ("m2", 3), ("m6", 0), ("m3", 3), ("m5", 1),
    ("m2", 2), ("a1", 0, 0), ("m6", 1), ("a1", 0, 1), ("m5", 3), ("m3", 2), ("a2", 0, 0), ("a1", 0, 2), ("a1", 1, 2),
    ("a1", 1, 0), ("m6", 3), ("m5", 2), ("a1", 1, 1), ("a2", 0, 1), ("acc", 0, 0, 0), ("a2", 1, 0), ("m6", 2),
    ("a2", 1, 2), ("acc", 0, 0, 1), ("acc", 0, 0, 2), ("a1", 3, 2), ("a1", 3, 0), ("a2", 0, 2), ("acc", 0, 1, 0),
    ("a1", 2, 2), ("a1", 2, 0), ("acc", 1, 0, 0), ("a2", 1, 1), ("a1", 2, 1), ("a1", 3, 1), ("a2", 3, 2),
    ("acc", 1, 0, 2), ("a2", 3, 0), ("acc", 1, 0, 1), ("a2", 2, 2), ("a2", 2, 0), ("acc", 0, 1, 2), ("a2", 2, 1),
    ("a2", 3, 1), ("acc", 0, 1, 1), ("acc", 1, 1, 0), ("acc", 1, 1, 2), ("acc", 1, 1, 1),
)


def flip4(v, bits):
    return (v, v + 1 - 2 * lax.rem(v, 2), 3 - v, lax.rem(v + 2, 4))[bits]


def cmp_at(c, j):
    y = lax.rem(c, 4)
    base = c - y
    return (4 - base if j & 4 else base) + flip4(y, j & 3)


def tgt_at(t, k):
    x, z, core = t // 4, lax.rem(t // 2, 2), lax.rem(t, 2)
    z = 1 - z if k & 4 else z
    core = 1 - core if k & 8 else core
    return flip4(x, k & 3) * 4 + z * 2 + core


def block_of(dims, r):
    return (dims[0] if r & 4 else 0) + (dims[1] if r & 2 else 0) + (dims[2] if r & 1 else 0)


def dim_of(dims, r):
    return dims[0 if r & 4 else 1 if r & 2 else 2]


def kernel(
    y_hbm, vc_hbm, vt_hbm, lc_ref, lt_ref, acc0, acc1, acc2, tfar, vcfar,
    y, vc, vct, vt, vtt, den, psend, precv, wown, qsend, qown, qrecv, q2send, q2recv, s, tbuf,
    in_sem, p_ss, p_rs, c_ss, c_rs, q_ss, q_rs, s_ss, s_rs, d_ss, d_rs, t_ss, t_rs,
):
    acc = (acc0, acc1, acc2)
    c, t = lax.axis_index("cmp"), lax.axis_index("tgt")
    rows, cols = y.shape[1], y.shape[2]
    kb = vc.shape[1] // 8
    kcs = kb // CHUNKS
    half = kb // 2
    tb = vt.shape[1] // 16

    cmp_peer = {d: {"cmp": cmp_at(c, d), "tgt": t} for d in (1, 2, 4)}
    tgt_peer = {k: {"cmp": c, "tgt": tgt_at(t, k)} for k in range(1, 9)}

    def remote(src, dst, ss, rs, peer):
        return pltpu.make_async_remote_copy(
            src_ref=src, dst_ref=dst, send_sem=ss, recv_sem=rs, device_id=peer, device_id_type=MESH
        )

    barrier = pltpu.get_barrier_semaphore()
    for peer in list(cmp_peer.values()) + list(tgt_peer.values()):
        pl.semaphore_signal(barrier, inc=1, device_id=peer, device_id_type=MESH)

    vc_in = {}
    for i in range(2):
        for j in range(8):
            vc_in[i, j] = pltpu.make_async_copy(
                vc_hbm.at[:, pl.ds(pl.multiple_of(cmp_at(c, j) * kb + i * half, half), half)],
                vc.at[:, pl.ds(j * kb + i * half, half)],
                in_sem.at[i * 8 + j],
            )
    y_in = [
        pltpu.make_async_copy(y_hbm.at[:, pl.ds(p * cols, cols)], y.at[p], in_sem.at[16 + p])
        for p in range(PARTS)
    ]
    vt_in = [
        pltpu.make_async_copy(
            vt_hbm.at[:, pl.ds(pl.multiple_of(tgt_at(t, k) * tb, tb), tb)],
            vt.at[:, pl.ds(k * tb, tb)],
            in_sem.at[19 + k],
        )
        for k in range(16)
    ]
    load_order = (7, 3, 5, 1, 6, 2, 4, 0)
    for j in load_order[:4]:
        vc_in[0, j].start()
    y_in[0].start()
    for j in load_order[4:]:
        vc_in[0, j].start()
    y_in[1].start()
    y_in[2].start()
    for j in load_order:
        vc_in[1, j].start()
    for copy in vt_in:
        copy.start()

    def transpose(i, js):
        for j in js:
            vc_in[i, j].wait()
            at = pl.ds(j * kb + i * half, half)
            vct[at, :] = vc[:, at].T

    def p_copy(h, p, r):
        return remote(
            psend.at[h, p, r - 1], precv.at[h, p, r - 1], p_ss.at[h, p, r - 1], p_rs.at[h, p, r - 1],
            cmp_peer[dim_of(SUM_DIMS[p], r)],
        )

    def got(h, p, r):
        p_copy(h, p, r).wait_recv()
        return precv[h, p, r - 1].astype(F32)

    def pc(h, p):
        lhs = [
            vct[pl.ds(block_of(SUM_DIMS[p], r) * kb + h * kcs, kcs), :] for r in range(7, -1, -1)
        ]
        prod = jnp.dot(jnp.concatenate(lhs, axis=0), y[p], preferred_element_type=F32)
        for i, r in enumerate(range(7, -1, -1)):
            block = prod[i * kcs : (i + 1) * kcs]
            if r >= 4:
                psend[h, p, r - 1] = block.astype(BF16)
            else:
                wown[h, p, r] = block

    def ps(h, p):
        p_copy(h, p, 7).start()
        p_copy(h, p, 6).start()

    def pt(h, p):
        p_copy(h, p, 5).start()
        p_copy(h, p, 4).start()

    def p2(h, p):
        for r in (3, 2):
            psend[h, p, r - 1] = (wown[h, p, r] + got(h, p, r + 4)).astype(BF16)
            p_copy(h, p, r).start()

    def p3(h, p):
        psend[h, p, 0] = (wown[h, p, 1] + got(h, p, 5) + got(h, p, 3)).astype(BF16)
        p_copy(h, p, 1).start()

    def c_copy(h):
        return remote(qsend.at[h], qrecv.at[h], c_ss.at[h], c_rs.at[h], tgt_peer[8])

    def pf(h):
        w = jnp.concatenate(
            [wown[h, p, 0] + got(h, p, 4) + got(h, p, 2) + got(h, p, 1) for p in range(PARTS)], axis=1
        )
        high = w.astype(BF16)
        low = (w - high.astype(F32)).astype(BF16)
        both = jnp.concatenate([high, low], axis=0)
        for k in (8, 10, 12, 14, 0, 2, 4, 6):
            q = jnp.dot(both, vt[:, k * tb : (k + 2) * tb], preferred_element_type=F32)
            q = q[:kcs] + q[kcs:]
            for i in range(2):
                block = q[:, i * tb : (i + 1) * tb]
                if k >= 8:
                    qsend[h, k - 8 + i] = block
                else:
                    qown[h, k + i] = block
            if k == 14:
                c_copy(h).start()

    def q_copy(h, k):
        if k == 4:
            return remote(q2send.at[h, 3], q2recv.at[h, 3], q_ss.at[h, 3], q_rs.at[h, 3], tgt_peer[4])
        return remote(q2send.at[h, k - 1], q2recv.at[h, k - 1], q_ss.at[h, k - 1], q_rs.at[h, k - 1], tgt_peer[k & 3])

    def m1(h):
        c_copy(h).wait_recv()
        for k in (7, 3, 5, 6, 1, 2):
            q2send[h, k - 1] = qown[h, k] + qrecv[h, k]
            q_copy(h, k).start()

    def m2(h):
        total = qown[h, 4] + qrecv[h, 4]
        for k in (5, 6, 7):
            q_copy(h, k).wait_recv()
            total += q2recv[h, k - 1]
        q2send[h, 3] = total
        q_copy(h, 4).start()
        total = qown[h, 0] + qrecv[h, 0]
        for k in (1, 2, 3):
            q_copy(h, k).wait_recv()
            total += q2recv[h, k - 1]
        qown[h, 0] = total

    def s_copy(h, k):
        return remote(s.at[h, 0, 0], s.at[h, 0, k], s_ss.at[h, k - 1], s_rs.at[h, k - 1], tgt_peer[k])

    def m3(h):
        q_copy(h, 4).wait_recv()
        total = qown[h, 0] + q2recv[h, 3]
        s[h, 0, 0] = (total / den[h * kcs : (h + 1) * kcs, :]).astype(BF16)
        for k in (7, 3, 5, 6, 1, 2, 4):
            s_copy(h, k).start()

    def d_copy(h):
        return remote(s.at[h, 0], s.at[h, 1], d_ss.at[h], d_rs.at[h], tgt_peer[8])

    def m5(h):
        for k in range(1, 8):
            s_copy(h, k).wait_recv()
        d_copy(h).start()

    def t_copy(h, p, r):
        d = 4 if r & 4 else 2 if r & 2 else 1
        return remote(
            tbuf.at[h, p, r - d], tbuf.at[h, p, r], t_ss.at[h, p, r - 1], t_rs.at[h, p, r - 1],
            cmp_peer[dim_of(GATHER_DIMS[p], r)],
        )

    def m6(h):
        d_copy(h).wait_recv()
        lhs = jnp.concatenate([s[h, i, k] for i in range(2) for k in range(8)], axis=1)
        part = jnp.dot(lhs, vtt[...], preferred_element_type=F32).astype(BF16)
        for p in range(PARTS):
            tbuf[h, p, 0] = part[:, p * cols : (p + 1) * cols]
        for r in (1, 2, 4):
            for p in range(PARTS):
                t_copy(h, p, r).start()

    def a1(h, p):
        t_copy(h, p, 1).wait_recv()
        t_copy(h, p, 2).wait_recv()
        for r in (3, 5, 6):
            t_copy(h, p, r).start()

    def a2(h, p):
        t_copy(h, p, 3).wait_recv()
        t_copy(h, p, 7).start()

    per_half = CHUNKS // 2

    def acc_step(i, far, p):
        chunks = range(i * per_half, (i + 1) * per_half)
        group = (3, 5, 6, 7) if far else (0, 1, 2, 4)
        for h in chunks:
            for r in group:
                if r >= 4:
                    t_copy(h, p, r).wait_recv()
        if i and far:
            for r in group:
                n = FAR.index(block_of(GATHER_DIMS[p], r))
                for h in chunks:
                    at = pl.ds(n * half + (h - chunks[0]) * kcs, kcs)
                    tfar[p, at, :] = tbuf[h, p, r]
            return
        first = not (i or far)
        rhs = jnp.concatenate([tbuf[h, p, r] for r in group for h in chunks], axis=0)

        @pl.loop(0, rows // ROW_TILE)
        def _(n):
            at = pl.ds(pl.multiple_of(n * ROW_TILE, ROW_TILE), ROW_TILE)
            lhs = jnp.concatenate(
                [vc[at, pl.ds(block_of(GATHER_DIMS[p], r) * kb + i * half, half)] for r in group], axis=1
            )
            prod = jnp.dot(lhs, rhs, preferred_element_type=F32)
            acc[p][at, :] = prod if first else acc[p][at, :] + prod

    def setup():
        den[...] = (
            jnp.broadcast_to(lc_ref[...], (tb, kb)).T * jnp.broadcast_to(lt_ref[...], (kb, tb)) + 0.25
        )
        for copy in vt_in:
            copy.wait()
        vtt[...] = vt[...].T
        for n, j in enumerate(FAR):
            vc_in_far = vc[:, pl.ds(j * kb + half, half)]
            vcfar[:, pl.ds(n * half, half)] = vc_in_far

    transpose(0, load_order)
    for p in range(PARTS):
        y_in[p].wait()
        pc(0, p)
    pl.semaphore_wait(barrier, len(cmp_peer) + len(tgt_peer))

    steps = {
        "tr": lambda n: transpose(1, (load_order[n],)), "setup": setup, "pc": pc, "ps": ps, "pt": pt,
        "p2": p2, "p3": p3, "pf": pf, "m1": m1, "m2": m2, "m3": m3, "m5": m5, "m6": m6, "a1": a1,
        "a2": a2, "acc": acc_step,
    }
    for name, *where in STEPS:
        steps[name](*where)

    for h in range(CHUNKS):
        c_copy(h).wait_send()
        d_copy(h).wait_send()
        for r in range(1, 8):
            q_copy(h, r).wait_send()
            s_copy(h, r).wait_send()
            for p in range(PARTS):
                p_copy(h, p, r).wait_send()
                t_copy(h, p, r).wait_send()


def finish(acc0, acc1, acc2, tfar, vcfar, out_hbm, buf, sem):
    acc = (acc0, acc1, acc2)
    rows, cols = acc0.shape
    copies = []
    for n in range(rows // LAST_TILE):
        at = pl.ds(n * LAST_TILE, LAST_TILE)
        for p in range(PARTS):
            prod = jnp.dot(vcfar[at, :], tfar[p], preferred_element_type=F32)
            buf[at, pl.ds(p * cols, cols)] = acc[p][at, :] + prod
        copy = pltpu.make_async_copy(buf.at[at], out_hbm.at[at], sem.at[n])
        copy.start()
        copies.append(copy)
    for copy in copies:
        copy.wait()


def shards(affinity, comp_vectors, targ_vectors, comp_values, targ_values):
    rows, targets = affinity.shape
    kc, kt = comp_vectors.shape[1], targ_vectors.shape[1]
    cols, kb, tb = targets // PARTS, kc // 8, kt // 16
    n, kcs = CHUNKS, kb // CHUNKS
    any_space = pl.BlockSpec(memory_space=pl.ANY)
    vmem = pl.BlockSpec(memory_space=pltpu.VMEM)
    dma = pltpu.SemaphoreType.DMA
    partial = pl.pallas_call(
        kernel,
        out_shape=[
            *[jax.ShapeDtypeStruct((rows, cols), F32)] * PARTS,
            jax.ShapeDtypeStruct((PARTS, 2 * kb, cols), BF16),
            jax.ShapeDtypeStruct((rows, 2 * kb), BF16),
        ],
        in_specs=[any_space, any_space, any_space, vmem, vmem],
        out_specs=[vmem] * (PARTS + 2),
        scratch_shapes=[
            pltpu.VMEM((PARTS, rows, cols), BF16),
            pltpu.VMEM((rows, kc), BF16),
            pltpu.VMEM((kc, rows), BF16),
            pltpu.VMEM((targets, kt), BF16),
            pltpu.VMEM((kt, targets), BF16),
            pltpu.VMEM((kb, tb), F32),
            pltpu.VMEM((n, PARTS, 7, kcs, cols), BF16),
            pltpu.VMEM((n, PARTS, 7, kcs, cols), BF16),
            pltpu.VMEM((n, PARTS, 4, kcs, cols), F32),
            pltpu.VMEM((n, 8, kcs, tb), F32),
            pltpu.VMEM((n, 8, kcs, tb), F32),
            pltpu.VMEM((n, 8, kcs, tb), F32),
            pltpu.VMEM((n, 7, kcs, tb), F32),
            pltpu.VMEM((n, 7, kcs, tb), F32),
            pltpu.VMEM((n, 2, 8, kcs, tb), BF16),
            pltpu.VMEM((n, PARTS, 8, kcs, cols), BF16),
            dma((35,)),
            dma((n, PARTS, 7)),
            dma((n, PARTS, 7)),
            dma((n,)),
            dma((n,)),
            dma((n, 7)),
            dma((n, 7)),
            dma((n, 7)),
            dma((n, 7)),
            dma((n,)),
            dma((n,)),
            dma((n, PARTS, 7)),
            dma((n, PARTS, 7)),
        ],
        compiler_params=pltpu.CompilerParams(
            collective_id=0, has_side_effects=True, vmem_limit_bytes=45 << 20
        ),
    )(affinity, comp_vectors, targ_vectors, comp_values[None, :], targ_values[None, :])
    return pl.pallas_call(
        finish,
        out_shape=jax.ShapeDtypeStruct((rows, targets), F32),
        in_specs=[vmem] * (PARTS + 2),
        out_specs=any_space,
        scratch_shapes=[pltpu.VMEM((rows, targets), F32), dma((rows // LAST_TILE,))],
        compiler_params=pltpu.CompilerParams(vmem_limit_bytes=8 << 20),
    )(*partial)


def solution(mesh):
    in_specs = (P("cmp", "tgt"), P("cmp", None), P("tgt", None), P("cmp"), P("tgt"))
    out_specs = P("cmp", "tgt")
    return jax.shard_map(shards, mesh=mesh, in_specs=in_specs, out_specs=out_specs, check_vma=False)
```
